32 devices in a mesh: groups: 2 (over y), gx: 4 (over z), gy: 2 (over x), gz: 2 (over core).
Axes of the slice: x: 2, y: 2, z: 4, core: 2. Of those that a mesh axis runs over, the one named last changes fastest.
Arguments:
- prompt_rows: bfloat16 [1024, 8192], P(('groups', 'gx', 'gz'), 'gy'), parts along dimension 0, may hold values from -6 to 6
- gate_up: bfloat16 [8192, 2, 28672], P('gy', None, ('gx', 'gz')), may hold values from -0.0625 to 0.0625
- queries: bfloat16 [2, 128, 8192], P(None, ('groups', 'gy'), ('gx', 'gz')), parts along dimension 1, may hold values from -128 to 128
- new_kv: bfloat16 [2, 128, 1024], P(None, ('groups', 'gy')), parts along dimension 1, may hold values from -6 to 6
- kv_cache: bfloat16 [128, 2048, 1024], P(('groups', 'gy'), ('gx', 'gz')), parts along dimension 0, may hold values from -6 to 6
- lengths: int32 [128], P(('groups', 'gy')), parts along dimension 0, may hold values from 2 to 2048, as said below
Outputs:
- hidden_units: bfloat16 [1024, 28672], P(('groups', 'gy'), ('gx', 'gz')), parts along dimension 0
- attended: bfloat16 [2, 128, 8192], P(None, ('groups', 'gy'), ('gx', 'gz')), parts along dimension 1
The draws below stay inside these ranges and needn't reach their ends.
There are 2 independent parts, one for each index of `groups`. The reference program is written for one: setup_inputs(seed, part) draws one part's arguments, and reference() takes and returns one part's arrays. A program takes and returns all parts, laid end to end along the dimension named above; an argument that names none is the same for every part. Nothing has to cross between parts.
Inputs may be any that keep to these rules, and one draw needn't show every extreme that they name: Slots 0 to lengths[b] - 1 of sequence b are live; some sequence has exactly 2048.
All inputs are finite; a program needn't handle non-finite values.
Results may differ from the reference program's by a relative error of at most 0.024.
Values may be sent and summed in bfloat16 or wider, within the bound.
A program may use at most 256 MiB of HBM per device.

```python
import math
import jax
import jax.numpy as jnp
from jax import lax

DW = 8192
FW = 28672
H = 64
KVH = 4
HD = 128
S = 2
B = 64
P_SIZE = 512
L = 2048
N_GY = 2


def front_slots(key):
    base_key = jax.random.fold_in(key, 12)
    leading = jnp.clip(jax.random.normal(base_key, (B, 2, 2, KVH, HD), jnp.float32), -6.0, 6.0)
    return leading


def draw_kv_cache(key, part):
    leading = front_slots(key)
    later_key = jax.random.fold_in(key, 13)
    remainder = jnp.clip(jax.random.normal(later_key, (B, L - 2, 2, KVH, HD), jnp.float32), -6.0, 6.0)
    complete = jnp.concatenate([leading, remainder], axis=1)
    return complete.reshape(B, L, 2 * KVH * HD).astype(jnp.bfloat16)


def draw_queries(key, part):
    drawn = jnp.clip(jax.random.normal(jax.random.fold_in(key, 14), (S, B, H * HD), jnp.float32), -6.0, 6.0)
    return drawn.astype(jnp.bfloat16)


def draw_lengths(key, part):
    base_key = jax.random.fold_in(key, 21)
    spread = jax.random.randint(jax.random.fold_in(base_key, 1), (B,), 2, L + 1)
    shorter = jax.random.randint(jax.random.fold_in(base_key, 2), (B,), 2, 17)
    picker = jax.random.randint(jax.random.fold_in(base_key, 3), (B,), 0, 8)
    chosen = jnp.where(picker == 0, shorter, spread)
    longest = jax.random.randint(jax.random.fold_in(base_key, 4), (), 0, B)
    return chosen.at[longest].set(L).astype(jnp.int32)


def level_of(key, dims, cuts, low, high):
    level, own = 1.0, jax.random.fold_in(key, 6)
    for axis_at, blocks in cuts:
        heights = jnp.exp(jax.random.uniform(jax.random.fold_in(own, axis_at), (blocks,), jnp.float32, low / len(cuts), high / len(cuts)))
        level = level * jnp.repeat(heights, dims[axis_at] // blocks).reshape([-1 if axis == axis_at else 1 for axis in range(len(dims))])
    return level


def bell_draw(key, shape, deviation, bound, split=(), kind=jnp.bfloat16):
    loudness = level_of(key, shape, split, -0.22, 0.18) if split else 1.0
    values = jax.random.normal(key, shape, jnp.float32) * deviation * loudness
    return jnp.minimum(jnp.maximum(values, -bound), bound).astype(kind)


def setup_inputs(seed: int = 0, part: int = 0) -> dict:
    key_list = jax.random.split(jax.random.key(seed), 7)
    own_keys = jax.random.split(jax.random.fold_in(key_list[6], part), 7)
    return {
        "prompt_rows": bell_draw(own_keys[0], (P_SIZE, DW), 1.0, 6.0, ((0, 8), (1, 2))),
        "gate_up": bell_draw(key_list[1], (DW, 2, FW), DW ** -0.5, 0.0625, ((0, 2), (2, 8))),
        "queries": draw_queries(jax.random.fold_in(jax.random.fold_in(key_list[6], part), 71), part),
        "new_kv": bell_draw(own_keys[3], (S, B, 2 * KVH * HD), 1.0, 6.0, ((1, 2),)),
        "kv_cache": draw_kv_cache(jax.random.fold_in(jax.random.fold_in(key_list[6], part), 71), part),
        "lengths": draw_lengths(jax.random.fold_in(jax.random.fold_in(key_list[6], part), 71), part),
    }


def one_sequence(inputs):
    seq_queries, fresh_kv, cache_rows, length = inputs
    combined = jnp.concatenate([cache_rows, fresh_kv], axis=0).reshape(L + S, 2, KVH, HD)
    key_rows = combined[:, 0].astype(jnp.float32)
    value_rows = combined[:, 1].astype(jnp.float32)
    grouped = seq_queries.reshape(S, KVH, H // KVH, HD).astype(jnp.float32)
    scores = jnp.einsum('skgd,jkd->skgj', grouped, key_rows) * (1.0 / math.sqrt(HD))
    position = jnp.arange(L + S, dtype=jnp.int32)
    step_ids = jnp.arange(S, dtype=jnp.int32)
    visible = (position[None, :] < length) | (position[None, :] >= L) & (position[None, :] - L <= step_ids[:, None])
    masked = jnp.where(visible[:, None, None, :], scores, -jnp.inf)
    row_max = lax.optimization_barrier(jnp.max(masked, axis=-1, keepdims=True))
    probabilities = jnp.exp(masked - row_max)
    denominator = lax.optimization_barrier(jnp.sum(probabilities, axis=-1, keepdims=True))
    weights = lax.optimization_barrier(probabilities.astype(jnp.bfloat16)).astype(jnp.float32)
    numerator = jnp.einsum('skgj,jkd->skgd', weights, value_rows)
    return (numerator / denominator).reshape(S, H * HD).astype(jnp.bfloat16)

def reference(prompt_rows, gate_up, queries, new_kv, kv_cache, lengths):
    block_width = DW // N_GY
    flat_weights = gate_up.reshape(DW, 2 * FW)
    summed = jnp.zeros((prompt_rows.shape[0], 2 * FW), jnp.float32)
    for member in range(N_GY):
        lower = member * block_width
        partial_value = jnp.dot(prompt_rows[:, lower:lower + block_width], flat_weights[lower:lower + block_width], preferred_element_type=jnp.float32)
        rounded = lax.optimization_barrier(partial_value.astype(jnp.bfloat16))
        summed = summed + rounded.astype(jnp.float32)
    summed = summed.reshape(-1, 2, FW)
    hidden_units = (jax.nn.silu(summed[:, 0]) * summed[:, 1]).astype(jnp.bfloat16)
    attended = lax.map(one_sequence, (jnp.transpose(queries, (1, 0, 2)), jnp.transpose(new_kv, (1, 0, 2)), kv_cache, lengths))
    return (hidden_units, jnp.transpose(attended, (1, 0, 2)))
```

```python
import functools
import math

import jax
import jax.numpy as jnp
from jax import lax
from jax.experimental import pallas as pl
from jax.experimental.pallas import tpu as pltpu
from jax.sharding import PartitionSpec as P

KVH = 4
HD = 128
MESH = pl.DeviceIdType.MESH

lowest = -1e30


def gather_kernel(Z, C, N, x_ref, out_ref, own_sem, rs, rr, ls, lr, xs, xr):
    z = lax.axis_index("gx")
    c = lax.axis_index("gz")
    y = lax.axis_index("gy")
    n = Z * C
    rows = x_ref.shape[0]

    def place(zz, cc):
        p = lax.rem(zz * C + cc - (y + 1) * (n // N) + 2 * n, n)
        return out_ref.at[pl.ds(pl.multiple_of(p * rows, rows), rows)]

    def right(k):
        src = x_ref if k == 0 else place(z - k, c)
        return pltpu.make_async_remote_copy(
            src_ref=src, dst_ref=place(z - k, c), send_sem=rs.at[k], recv_sem=rr.at[k],
            device_id={"gx": z + 1}, device_id_type=MESH)

    def left(k):
        src = x_ref if k == 0 else place(z + k, c)
        return pltpu.make_async_remote_copy(
            src_ref=src, dst_ref=place(z + k, c), send_sem=ls.at[k], recv_sem=lr.at[k],
            device_id={"gx": z - 1}, device_id_type=MESH)

    def right_in(k):
        return pltpu.make_async_remote_copy(
            src_ref=x_ref, dst_ref=place(z - 1 - k, c), send_sem=rs.at[k], recv_sem=rr.at[k],
            device_id={"gx": z - 1}, device_id_type=MESH)

    def left_in(k):
        return pltpu.make_async_remote_copy(
            src_ref=x_ref, dst_ref=place(z + 1 + k, c), send_sem=ls.at[k], recv_sem=lr.at[k],
            device_id={"gx": z + 1}, device_id_type=MESH)

    def cross(zz, slot, src=None):
        block = place(zz, c)
        return pltpu.make_async_remote_copy(
            src_ref=block if src is None else src, dst_ref=block,
            send_sem=xs.at[slot], recv_sem=xr.at[slot],
            device_id={"gz": 1 - c}, device_id_type=MESH)

    def cross_in(zz, slot):
        return pltpu.make_async_remote_copy(
            src_ref=x_ref, dst_ref=place(zz, 1 - c),
            send_sem=xs.at[slot], recv_sem=xr.at[slot],
            device_id={"gz": 1 - c}, device_id_type=MESH)

    barrier = pltpu.get_barrier_semaphore()

    @pl.when(z < Z - 1)
    def _():
        pl.semaphore_signal(barrier, inc=1, device_id={"gx": z + 1}, device_id_type=MESH)

    @pl.when(z > 0)
    def _():
        pl.semaphore_signal(barrier, inc=1, device_id={"gx": z - 1}, device_id_type=MESH)

    pl.semaphore_signal(barrier, inc=1, device_id={"gz": 1 - c}, device_id_type=MESH)
    peers = 1 + (z > 0).astype(jnp.int32) + (z < Z - 1).astype(jnp.int32)
    pl.semaphore_wait(barrier, peers)

    own = pltpu.make_async_copy(x_ref, place(z, c), own_sem)

    for k in range(Z - 1):
        @pl.when((z < Z - 1) & (z - k >= 0))
        def _():
            right(k).start()

        @pl.when((z > 0) & (z + k < Z))
        def _():
            left(k).start()

        if k == 0:
            own.start()
            cross(z, 0, x_ref).start()

        @pl.when(z - 1 - k >= 0)
        def _():
            right_in(k).wait_recv()
            cross(z - 1 - k, 1 + k).start()

        @pl.when(z + 1 + k < Z)
        def _():
            left_in(k).wait_recv()
            cross(z + 1 + k, Z + k).start()

    own.wait()
    cross(z, 0, x_ref).wait_send()
    cross_in(z, 0).wait_recv()
    for k in range(Z - 1):
        @pl.when((z < Z - 1) & (z - k >= 0))
        def _():
            right(k).wait_send()

        @pl.when((z > 0) & (z + k < Z))
        def _():
            left(k).wait_send()

        @pl.when(z - 1 - k >= 0)
        def _():
            cross(z - 1 - k, 1 + k).wait_send()
            cross_in(z - 1 - k, 1 + k).wait_recv()

        @pl.when(z + 1 + k < Z)
        def _():
            cross(z + 1 + k, Z + k).wait_send()
            cross_in(z + 1 + k, Z + k).wait_recv()


def gather_prompt(x):
    Z, C, N = lax.axis_size("gx"), lax.axis_size("gz"), lax.axis_size("gy")
    rows, depth = x.shape
    sems = pltpu.SemaphoreType.DMA((Z - 1,))
    cross_sems = pltpu.SemaphoreType.DMA((2 * Z - 1,))
    return pl.pallas_call(
        functools.partial(gather_kernel, Z, C, N),
        out_shape=jax.ShapeDtypeStruct((Z * C * rows, depth), x.dtype),
        in_specs=[pl.BlockSpec(memory_space=pl.ANY)],
        out_specs=pl.BlockSpec(memory_space=pltpu.VMEM),
        scratch_shapes=[pltpu.SemaphoreType.DMA, sems, sems, sems, sems, cross_sems, cross_sems],
        compiler_params=pltpu.CompilerParams(collective_id=0, has_side_effects=True),
        name="gather_prompt",
    )(x)


def attention_kernel(scale, lens_ref, offset_ref, q_ref, kv_ref, num_ref, stat_ref):
    step = pl.program_id(0)
    per_step, slots, width = kv_ref.shape
    half = width // 2
    wide = q_ref.shape[1]
    per_head = wide // KVH
    row = lax.broadcasted_iota(jnp.int32, (wide, half), 0) // per_head
    col = lax.broadcasted_iota(jnp.int32, (wide, half), 1) // HD
    same = row == col
    position = offset_ref[0] + lax.broadcasted_iota(jnp.int32, (slots, wide), 0)
    for i in range(per_step):
        q = q_ref[i]
        spread = jnp.where(same, jnp.concatenate([q] * KVH, axis=1), jnp.zeros((), q.dtype))
        scores = lax.dot_general(
            kv_ref[i, :, :half], spread, (((1,), (1,)), ((), ())),
            preferred_element_type=jnp.float32) * scale
        visible = position < lens_ref[step * per_step + i]
        masked = jnp.where(visible, scores, lowest)
        top = jnp.max(masked, axis=0, keepdims=True)
        probs = jnp.where(visible, jnp.exp(masked - top), 0.0)
        stat_ref[i, 0:1, :] = top
        stat_ref[i, 1:2, :] = jnp.sum(probs, axis=0, keepdims=True)
        full = lax.dot_general(
            probs.astype(jnp.bfloat16), kv_ref[i, :, half:], (((0,), (0,)), ((), ())),
            preferred_element_type=jnp.float32)
        for g in range(KVH):
            lo = g * per_head
            num_ref[i, lo:lo + per_head, :] = full[
                lo:lo + per_head, g * HD:(g + 1) * HD].astype(num_ref.dtype)


def attention(q, kv, lengths, offset):
    sequences, slots, width = kv.shape
    wide = q.shape[1]
    per_step = 4 if sequences % 4 == 0 else 1
    return pl.pallas_call(
        functools.partial(attention_kernel, 1.0 / math.sqrt(HD)),
        out_shape=(
            jax.ShapeDtypeStruct((sequences, wide, HD), jnp.bfloat16),
            jax.ShapeDtypeStruct((sequences, 2, wide), jnp.float32),
        ),
        grid_spec=pltpu.PrefetchScalarGridSpec(
            num_scalar_prefetch=2,
            grid=(sequences // per_step,),
            in_specs=[
                pl.BlockSpec((per_step, wide, HD), lambda i, a, b: (i, 0, 0)),
                pl.BlockSpec((per_step, slots, width), lambda i, a, b: (i, 0, 0)),
            ],
            out_specs=[
                pl.BlockSpec((per_step, wide, HD), lambda i, a, b: (i, 0, 0)),
                pl.BlockSpec((per_step, 2, wide), lambda i, a, b: (i, 0, 0)),
            ],
        ),
        cost_estimate=pl.CostEstimate(
            flops=sequences * slots * wide * width * 2,
            bytes_accessed=sequences * slots * width * 2,
            transcendentals=sequences * slots * wide),
        name="slot_attention",
    )(lengths, offset, q, kv)


def shifted(x, axes, k):
    n = lax.axis_size(axes)
    return lax.ppermute(x, axes, [(i, (i + k) % n) for i in range(n)])


def chunk_sizes(columns):
    tiles, sizes, step = columns // 128, [], 2
    while tiles >= step:
        sizes.append(step)
        tiles -= step
        step += 1
    sizes[-1] += tiles
    sizes = sizes[0::2] + sizes[1::2][::-1]
    return [128 * size for size in sizes]


def projections(x_all, gate_up, between):
    N = lax.axis_size("gy")
    rows = x_all.shape[0] // N
    sizes = chunk_sizes(gate_up.shape[2])
    x_keep = x_all[(N - 1) * rows:]

    def product(x, c):
        lo = sum(sizes[:c])
        part = lax.dot_general(
            x, gate_up[:, :, lo:lo + sizes[c]], (((1,), (0,)), ((), ())),
            preferred_element_type=jnp.float32)
        return jnp.transpose(part, (1, 0, 2)).astype(jnp.bfloat16)

    arrived = []
    for c in range(len(sizes)):
        parts = [product(x_all[(k - 1) * rows:k * rows], c) for k in range(1, N)]
        arrived.append([shifted(part, "gy", k + 1) for k, part in enumerate(parts)])
    x_keep, parts, between = lax.optimization_barrier((x_keep, parts, between))
    hidden = []
    for c in range(len(sizes)):
        total = product(x_keep, c).astype(jnp.float32)
        for other in arrived[c]:
            total = total + other.astype(jnp.float32)
        hidden.append((jax.nn.silu(total[0]) * total[1]).astype(jnp.bfloat16))
    return jnp.concatenate(hidden, axis=1), between


def on_device(prompt_rows, gate_up, queries, new_kv, kv_cache, lengths):
    both = ("gx", "gz")
    n = lax.axis_size(both)
    me = lax.axis_index(both)
    S, B, width = queries.shape
    heads = width // HD
    group = n * heads // KVH
    per = n // KVH

    x_all = gather_prompt(prompt_rows)
    x_all, late_queries = lax.optimization_barrier((x_all, queries))

    slots_of = jnp.zeros((n, S, B, width), queries.dtype)
    slots_of = lax.dynamic_update_index_in_dim(slots_of, late_queries, me, 0)
    for k in range(1, n):
        slots_of = lax.dynamic_update_index_in_dim(
            slots_of, shifted(late_queries, both, k), lax.rem(me - k + n, n), 0)
    q = slots_of.reshape(KVH, per, S, B, heads, HD)
    q = jnp.transpose(q, (3, 0, 2, 1, 4, 5)).reshape(B, KVH * S * group, HD)

    offset = (me * kv_cache.shape[1]).astype(jnp.int32).reshape(1)
    num, stat = attention(q, kv_cache, lengths, offset)
    hidden_units, (num, stat) = projections(x_all, gate_up, (num, stat))
    num = jnp.transpose(num.reshape(B, KVH, S, per, heads, HD), (1, 3, 2, 0, 4, 5))
    num = num.reshape(n, S, B, width)
    stat = jnp.transpose(stat.reshape(B, 2, KVH, S, per, heads), (2, 4, 1, 3, 0, 5))
    stat = stat.reshape(n, 2, S, B, heads)

    def take(a, i):
        return lax.dynamic_index_in_dim(a, i, 0, False)

    nums, stats = [take(num, me)], [take(stat, me)]
    for k in range(1, n):
        target = lax.rem(me + k, n)
        nums.append(shifted(take(num, target), both, k))
        stats.append(shifted(take(stat, target), both, k))

    head_at = me * heads // group
    fresh = new_kv.reshape(S, B, 2, KVH, HD)
    keys = lax.dynamic_index_in_dim(fresh[:, :, 0], head_at, 2, False).astype(jnp.float32)
    values = lax.dynamic_index_in_dim(fresh[:, :, 1], head_at, 2, False).astype(jnp.float32)
    mine = queries.reshape(S, B, heads, HD).astype(jnp.float32)
    scores = jnp.sum(mine[:, None] * keys[None, :, :, None, :], axis=-1) * (1.0 / math.sqrt(HD))
    steps = jnp.arange(S)
    seen = (steps[None, :] <= steps[:, None])[:, :, None, None]
    scores = jnp.where(seen, scores, lowest)
    top = jnp.max(scores, axis=1)
    for s in stats:
        top = jnp.maximum(top, s[0])
    probs = jnp.where(seen, jnp.exp(scores - top[:, None]), 0.0)
    denominator = jnp.sum(probs, axis=1)
    weights = probs.astype(jnp.bfloat16).astype(jnp.float32)
    numerator = jnp.sum(weights[..., None] * values[None, :, :, None, :], axis=1)
    for a, s in zip(nums, stats):
        scale = jnp.exp(s[0] - top)
        denominator = denominator + s[1] * scale
        numerator = numerator + a.reshape(S, B, heads, HD).astype(jnp.float32) * scale[..., None]
    attended = (numerator / denominator[..., None]).astype(jnp.bfloat16).reshape(S, B, width)
    return (hidden_units, attended)


def solution(mesh):
    return jax.shard_map(
        on_device,
        mesh=mesh,
        in_specs=(
            P(("groups", "gx", "gz"), "gy"),
            P("gy", None, ("gx", "gz")),
            P(None, ("groups", "gy"), ("gx", "gz")),
            P(None, ("groups", "gy"), None),
            P(("groups", "gy"), ("gx", "gz"), None),
            P(("groups", "gy")),
        ),
        out_specs=(P(("groups", "gy"), ("gx", "gz")), P(None, ("groups", "gy"), ("gx", "gz"))),
        check_vma=False,
    )
```

```python
import functools
import math

import jax
import jax.numpy as jnp
from jax import lax
from jax.experimental import pallas as pl
from jax.experimental.pallas import tpu as pltpu
from jax.sharding import PartitionSpec as P

KVH = 4
HD = 128
MESH = pl.DeviceIdType.MESH

lowest = -1e30


def gather_kernel(Z, C, N, sizes, x_ref, w_ref, out_ref, *rest):
    w_outs = rest[:len(sizes)]
    own_sem, rs, rr, ls, lr, xs, xr, buf, in_sems, out_sems = rest[len(sizes):]
    depth = buf.shape[1]
    cuts = w_ref.shape[0] // depth
    pieces = [(c, i) for c in range(len(sizes)) for i in range(cuts)]
    slots = buf.shape[0]

    def load(p):
        c, i = pieces[p]
        return pltpu.make_async_copy(
            w_ref.at[pl.ds(i * depth, depth), :, pl.ds(sum(sizes[:c]), sizes[c])],
            buf.at[p % slots, :, :, pl.ds(0, sizes[c])], in_sems.at[p])

    def save(p):
        c, i = pieces[p]
        return pltpu.make_async_copy(
            buf.at[p % slots, :, :, pl.ds(0, sizes[c])],
            w_outs[c].at[pl.ds(i * depth, depth)], out_sems.at[p])

    def split(first, last):
        for p in range(first, last):
            load(p).wait()
            save(p).start()
            if p >= 1:
                save(p - 1).wait()
            if p + slots - 1 < len(pieces):
                load(p + slots - 1).start()

    for p in range(min(slots - 1, len(pieces))):
        load(p).start()
    z = lax.axis_index("gx")
    c = lax.axis_index("gz")
    y = lax.axis_index("gy")
    n = Z * C
    rows = x_ref.shape[0]

    def place(zz, cc):
        p = lax.rem(zz * C + cc - (y + 1) * (n // N) + 2 * n, n)
        return out_ref.at[pl.ds(pl.multiple_of(p * rows, rows), rows)]

    def right(k):
        src = x_ref if k == 0 else place(z - k, c)
        return pltpu.make_async_remote_copy(
            src_ref=src, dst_ref=place(z - k, c), send_sem=rs.at[k], recv_sem=rr.at[k],
            device_id={"gx": z + 1}, device_id_type=MESH)

    def left(k):
        src = x_ref if k == 0 else place(z + k, c)
        return pltpu.make_async_remote_copy(
            src_ref=src, dst_ref=place(z + k, c), send_sem=ls.at[k], recv_sem=lr.at[k],
            device_id={"gx": z - 1}, device_id_type=MESH)

    def right_in(k):
        return pltpu.make_async_remote_copy(
            src_ref=x_ref, dst_ref=place(z - 1 - k, c), send_sem=rs.at[k], recv_sem=rr.at[k],
            device_id={"gx": z - 1}, device_id_type=MESH)

    def left_in(k):
        return pltpu.make_async_remote_copy(
            src_ref=x_ref, dst_ref=place(z + 1 + k, c), send_sem=ls.at[k], recv_sem=lr.at[k],
            device_id={"gx": z + 1}, device_id_type=MESH)

    def cross(zz, slot, src=None):
        block = place(zz, c)
        return pltpu.make_async_remote_copy(
            src_ref=block if src is None else src, dst_ref=block,
            send_sem=xs.at[slot], recv_sem=xr.at[slot],
            device_id={"gz": 1 - c}, device_id_type=MESH)

    def cross_in(zz, slot):
        return pltpu.make_async_remote_copy(
            src_ref=x_ref, dst_ref=place(zz, 1 - c),
            send_sem=xs.at[slot], recv_sem=xr.at[slot],
            device_id={"gz": 1 - c}, device_id_type=MESH)

    barrier = pltpu.get_barrier_semaphore()

    @pl.when(z < Z - 1)
    def _():
        pl.semaphore_signal(barrier, inc=1, device_id={"gx": z + 1}, device_id_type=MESH)

    @pl.when(z > 0)
    def _():
        pl.semaphore_signal(barrier, inc=1, device_id={"gx": z - 1}, device_id_type=MESH)

    pl.semaphore_signal(barrier, inc=1, device_id={"gz": 1 - c}, device_id_type=MESH)
    peers = 1 + (z > 0).astype(jnp.int32) + (z < Z - 1).astype(jnp.int32)
    pl.semaphore_wait(barrier, peers)

    own = pltpu.make_async_copy(x_ref, place(z, c), own_sem)

    for k in range(Z - 1):
        @pl.when((z < Z - 1) & (z - k >= 0))
        def _():
            right(k).start()

        @pl.when((z > 0) & (z + k < Z))
        def _():
            left(k).start()

        if k == 0:
            own.start()
            cross(z, 0, x_ref).start()

        split(k * len(pieces) // (Z - 1), (k + 1) * len(pieces) // (Z - 1))

        @pl.when(z - 1 - k >= 0)
        def _():
            right_in(k).wait_recv()
            cross(z - 1 - k, 1 + k).start()

        @pl.when(z + 1 + k < Z)
        def _():
            left_in(k).wait_recv()
            cross(z + 1 + k, Z + k).start()

    save(len(pieces) - 1).wait()
    own.wait()
    cross(z, 0, x_ref).wait_send()
    cross_in(z, 0).wait_recv()
    for k in range(Z - 1):
        @pl.when((z < Z - 1) & (z - k >= 0))
        def _():
            right(k).wait_send()

        @pl.when((z > 0) & (z + k < Z))
        def _():
            left(k).wait_send()

        @pl.when(z - 1 - k >= 0)
        def _():
            cross(z - 1 - k, 1 + k).wait_send()
            cross_in(z - 1 - k, 1 + k).wait_recv()

        @pl.when(z + 1 + k < Z)
        def _():
            cross(z + 1 + k, Z + k).wait_send()
            cross_in(z + 1 + k, Z + k).wait_recv()


def gather_prompt(x, gate_up):
    Z, C, N = lax.axis_size("gx"), lax.axis_size("gz"), lax.axis_size("gy")
    rows, depth = x.shape
    sizes = chunk_sizes(gate_up.shape[2])
    cut = gate_up.shape[0] // 4
    count = 4 * len(sizes)
    sems = pltpu.SemaphoreType.DMA((Z - 1,))
    cross_sems = pltpu.SemaphoreType.DMA((2 * Z - 1,))
    split_sems = pltpu.SemaphoreType.DMA((count,))
    out = pl.pallas_call(
        functools.partial(gather_kernel, Z, C, N, sizes),
        out_shape=[jax.ShapeDtypeStruct((Z * C * rows, depth), x.dtype)] + [
            jax.ShapeDtypeStruct((gate_up.shape[0], 2, size), gate_up.dtype) for size in sizes],
        in_specs=[pl.BlockSpec(memory_space=pl.ANY)] * 2,
        out_specs=[pl.BlockSpec(memory_space=pltpu.VMEM)] + [
            pl.BlockSpec(memory_space=pl.ANY)] * len(sizes),
        scratch_shapes=[
            pltpu.SemaphoreType.DMA, sems, sems, sems, sems, cross_sems, cross_sems,
            pltpu.VMEM((4, cut, 2, max(sizes)), gate_up.dtype), split_sems, split_sems],
        compiler_params=pltpu.CompilerParams(
            collective_id=0, has_side_effects=True, vmem_limit_bytes=40 * 2**20),
        name="gather_prompt",
    )(x, gate_up)
    return out[0], out[1:]


def attention_kernel(scale, lens_ref, offset_ref, q_ref, kv_ref, num_ref, stat_ref):
    step = pl.program_id(0)
    per_step, slots, width = kv_ref.shape
    half = width // 2
    wide = q_ref.shape[1]
    per_head = wide // KVH
    row = lax.broadcasted_iota(jnp.int32, (wide, half), 0) // per_head
    col = lax.broadcasted_iota(jnp.int32, (wide, half), 1) // HD
    same = row == col
    position = offset_ref[0] + lax.broadcasted_iota(jnp.int32, (slots, wide), 0)
    for i in range(per_step):
        q = q_ref[i]
        spread = jnp.where(same, jnp.concatenate([q] * KVH, axis=1), jnp.zeros((), q.dtype))
        scores = lax.dot_general(
            kv_ref[i, :, :half], spread, (((1,), (1,)), ((), ())),
            preferred_element_type=jnp.float32) * scale
        visible = position < lens_ref[step * per_step + i]
        masked = jnp.where(visible, scores, lowest)
        top = jnp.max(masked, axis=0, keepdims=True)
        probs = jnp.where(visible, jnp.exp(masked - top), 0.0)
        stat_ref[i, 0:1, :] = top
        stat_ref[i, 1:2, :] = jnp.sum(probs, axis=0, keepdims=True)
        full = lax.dot_general(
            probs.astype(jnp.bfloat16), kv_ref[i, :, half:], (((0,), (0,)), ((), ())),
            preferred_element_type=jnp.float32)
        for g in range(KVH):
            lo = g * per_head
            num_ref[i, lo:lo + per_head, :] = full[
                lo:lo + per_head, g * HD:(g + 1) * HD].astype(num_ref.dtype)


def attention(q, kv, lengths, offset):
    sequences, slots, width = kv.shape
    wide = q.shape[1]
    per_step = 4 if sequences % 4 == 0 else 1
    return pl.pallas_call(
        functools.partial(attention_kernel, 1.0 / math.sqrt(HD)),
        out_shape=(
            jax.ShapeDtypeStruct((sequences, wide, HD), jnp.bfloat16),
            jax.ShapeDtypeStruct((sequences, 2, wide), jnp.float32),
        ),
        grid_spec=pltpu.PrefetchScalarGridSpec(
            num_scalar_prefetch=2,
            grid=(sequences // per_step,),
            in_specs=[
                pl.BlockSpec((per_step, wide, HD), lambda i, a, b: (i, 0, 0)),
                pl.BlockSpec((per_step, slots, width), lambda i, a, b: (i, 0, 0)),
            ],
            out_specs=[
                pl.BlockSpec((per_step, wide, HD), lambda i, a, b: (i, 0, 0)),
                pl.BlockSpec((per_step, 2, wide), lambda i, a, b: (i, 0, 0)),
            ],
        ),
        cost_estimate=pl.CostEstimate(
            flops=sequences * slots * wide * width * 2,
            bytes_accessed=sequences * slots * width * 2,
            transcendentals=sequences * slots * wide),
        name="slot_attention",
    )(lengths, offset, q, kv)


def shifted(x, axes, k):
    n = lax.axis_size(axes)
    return lax.ppermute(x, axes, [(i, (i + k) % n) for i in range(n)])


def chunk_sizes(columns):
    tiles = columns // 128
    count = max(1, tiles // 4)
    sizes = [tiles // count] * count
    sizes[-1] += tiles - sum(sizes)
    return [128 * size for size in sizes]


def projections(x_all, weights, between):
    N = lax.axis_size("gy")
    rows = x_all.shape[0] // N
    chunks = range(len(weights))
    x_keep = x_all[(N - 1) * rows:]

    def product(x, c):
        part = lax.dot_general(
            x, weights[c], (((1,), (0,)), ((), ())),
            preferred_element_type=jnp.float32)
        return jnp.transpose(part, (1, 0, 2)).astype(jnp.bfloat16)

    arrived = []
    for c in chunks:
        parts = [product(x_all[(k - 1) * rows:k * rows], c) for k in range(1, N)]
        arrived.append([shifted(part, "gy", k + 1) for k, part in enumerate(parts)])
    x_keep, parts, between = lax.optimization_barrier((x_keep, parts, between))
    hidden = []
    for c in chunks:
        total = product(x_keep, c).astype(jnp.float32)
        for other in arrived[c]:
            total = total + other.astype(jnp.float32)
        hidden.append((jax.nn.silu(total[0]) * total[1]).astype(jnp.bfloat16))
    return jnp.concatenate(hidden, axis=1), between


def join_kernel(n, q_ref, k_ref, v_ref, *refs):
    num_refs, stat_refs, out_ref = refs[:n], refs[n:2 * n], refs[2 * n]
    S, B, width = q_ref.shape
    scale = 1.0 / math.sqrt(HD)
    for s in range(S):
        keys = [k_ref[t].astype(jnp.float32) for t in range(s + 1)]
        values = [v_ref[t].astype(jnp.float32) for t in range(s + 1)]
        for h in range(width // HD):
            lanes = slice(h * HD, (h + 1) * HD)
            q = q_ref[s, :, lanes].astype(jnp.float32)
            fresh = [jnp.sum(q * key, axis=-1, keepdims=True) * scale for key in keys]
            tops = [r[0, s, :, h:h + 1] for r in stat_refs]
            top = functools.reduce(jnp.maximum, fresh + tops)
            denominator = jnp.zeros_like(top)
            numerator = jnp.zeros_like(q)
            for score, value in zip(fresh, values):
                prob = jnp.exp(score - top)
                denominator = denominator + prob
                numerator = numerator + prob.astype(jnp.bfloat16).astype(jnp.float32) * value
            for local, num, stat in zip(tops, num_refs, stat_refs):
                factor = jnp.exp(local - top)
                denominator = denominator + stat[1, s, :, h:h + 1] * factor
                numerator = numerator + num[s, :, lanes].astype(jnp.float32) * factor
            out_ref[s, :, lanes] = (numerator / denominator).astype(out_ref.dtype)


def join(q, k, v, nums, stats):
    n = len(nums)
    return pl.pallas_call(
        functools.partial(join_kernel, n),
        out_shape=jax.ShapeDtypeStruct(q.shape, q.dtype),
        in_specs=[pl.BlockSpec(memory_space=pltpu.VMEM)] * (3 + 2 * n),
        out_specs=pl.BlockSpec(memory_space=pltpu.VMEM),
        cost_estimate=pl.CostEstimate(
            flops=8 * n * q.size, bytes_accessed=2 * (n + 2) * q.size, transcendentals=0),
        name="join_parts",
    )(q, k, v, *nums, *stats)


def on_device(prompt_rows, gate_up, queries, new_kv, kv_cache, lengths):
    both = ("gx", "gz")
    n = lax.axis_size(both)
    me = lax.axis_index(both)
    S, B, width = queries.shape
    heads = width // HD
    group = n * heads // KVH
    per = n // KVH

    x_all, weights = gather_prompt(prompt_rows, gate_up)
    x_all, late_queries = lax.optimization_barrier((x_all, queries))

    slots_of = jnp.zeros((n, S, B, width), queries.dtype)
    slots_of = lax.dynamic_update_index_in_dim(slots_of, late_queries, me, 0)
    for k in range(1, n):
        slots_of = lax.dynamic_update_index_in_dim(
            slots_of, shifted(late_queries, both, k), lax.rem(me - k + n, n), 0)
    q = slots_of.reshape(KVH, per, S, B, heads, HD)
    q = jnp.transpose(q, (3, 0, 2, 1, 4, 5)).reshape(B, KVH * S * group, HD)

    offset = (me * kv_cache.shape[1]).astype(jnp.int32).reshape(1)
    num, stat = attention(q, kv_cache, lengths, offset)
    hidden_units, (num, stat) = projections(x_all, weights, (num, stat))
    num = jnp.transpose(num.reshape(B, KVH, S, per, heads, HD), (1, 3, 2, 0, 4, 5))
    num = num.reshape(n, S, B, width)
    stat = jnp.transpose(stat.reshape(B, 2, KVH, S, per, heads), (2, 4, 1, 3, 0, 5))
    stat = stat.reshape(n, 2, S, B, heads)

    def take(a, i):
        return lax.dynamic_index_in_dim(a, i, 0, False)

    nums, stats = [take(num, me)], [take(stat, me)]
    for k in range(1, n):
        target = lax.rem(me + k, n)
        nums.append(shifted(take(num, target), both, k))
        stats.append(shifted(take(stat, target), both, k))

    head_at = me * heads // group
    fresh = new_kv.reshape(S, B, 2, KVH, HD)
    keys = lax.dynamic_index_in_dim(fresh[:, :, 0], head_at, 2, False)
    values = lax.dynamic_index_in_dim(fresh[:, :, 1], head_at, 2, False)
    attended = join(queries, keys, values, nums, stats)
    return (hidden_units, attended)


def solution(mesh):
    return jax.shard_map(
        on_device,
        mesh=mesh,
        in_specs=(
            P(("groups", "gx", "gz"), "gy"),
            P("gy", None, ("gx", "gz")),
            P(None, ("groups", "gy"), ("gx", "gz")),
            P(None, ("groups", "gy"), None),
            P(("groups", "gy"), ("gx", "gz"), None),
            P(("groups", "gy")),
        ),
        out_specs=(P(("groups", "gy"), ("gx", "gz")), P(None, ("groups", "gy"), ("gx", "gz"))),
        check_vma=False,
    )
```

```python
import functools
import math

import jax
import jax.numpy as jnp
from jax import lax
from jax.experimental import pallas as pl
from jax.experimental.pallas import tpu as pltpu
from jax.sharding import PartitionSpec as P

KVH = 4
HD = 128
MESH = pl.DeviceIdType.MESH

lowest = -1e30


def gather_kernel(Z, C, N, sizes, x_ref, w_ref, out_ref, *rest):
    w_outs = rest[:len(sizes)]
    own_sem, rs, rr, ls, lr, xs, xr, buf, in_sems, out_sems = rest[len(sizes):]
    depth = buf.shape[1]
    cuts = w_ref.shape[0] // depth
    pieces = [(c, i) for c in range(len(sizes)) for i in range(cuts)]
    slots = buf.shape[0]

    def load(p):
        c, i = pieces[p]
        return pltpu.make_async_copy(
            w_ref.at[pl.ds(i * depth, depth), :, pl.ds(sum(sizes[:c]), sizes[c])],
            buf.at[p % slots, :, :, pl.ds(0, sizes[c])], in_sems.at[p])

    def save(p):
        c, i = pieces[p]
        return pltpu.make_async_copy(
            buf.at[p % slots, :, :, pl.ds(0, sizes[c])],
            w_outs[c].at[pl.ds(i * depth, depth)], out_sems.at[p])

    def split(first, last):
        for p in range(first, last):
            load(p).wait()
            save(p).start()
            if p >= 1:
                save(p - 1).wait()
            if p + slots - 1 < len(pieces):
                load(p + slots - 1).start()

    for p in range(min(slots - 1, len(pieces))):
        load(p).start()
    z = lax.axis_index("gx")
    c = lax.axis_index("gz")
    y = lax.axis_index("gy")
    n = Z * C
    rows = x_ref.shape[0]

    def place(zz, cc):
        p = lax.rem(zz * C + cc - (y + 1) * (n // N) + 2 * n, n)
        return out_ref.at[pl.ds(pl.multiple_of(p * rows, rows), rows)]

    def right(k):
        src = x_ref if k == 0 else place(z - k, c)
        return pltpu.make_async_remote_copy(
            src_ref=src, dst_ref=place(z - k, c), send_sem=rs.at[k], recv_sem=rr.at[k],
            device_id={"gx": z + 1}, device_id_type=MESH)

    def left(k):
        src = x_ref if k == 0 else place(z + k, c)
        return pltpu.make_async_remote_copy(
            src_ref=src, dst_ref=place(z + k, c), send_sem=ls.at[k], recv_sem=lr.at[k],
            device_id={"gx": z - 1}, device_id_type=MESH)

    def right_in(k):
        return pltpu.make_async_remote_copy(
            src_ref=x_ref, dst_ref=place(z - 1 - k, c), send_sem=rs.at[k], recv_sem=rr.at[k],
            device_id={"gx": z - 1}, device_id_type=MESH)

    def left_in(k):
        return pltpu.make_async_remote_copy(
            src_ref=x_ref, dst_ref=place(z + 1 + k, c), send_sem=ls.at[k], recv_sem=lr.at[k],
            device_id={"gx": z + 1}, device_id_type=MESH)

    def cross(zz, slot, src=None):
        block = place(zz, c)
        return pltpu.make_async_remote_copy(
            src_ref=block if src is None else src, dst_ref=block,
            send_sem=xs.at[slot], recv_sem=xr.at[slot],
            device_id={"gz": 1 - c}, device_id_type=MESH)

    def cross_in(zz, slot):
        return pltpu.make_async_remote_copy(
            src_ref=x_ref, dst_ref=place(zz, 1 - c),
            send_sem=xs.at[slot], recv_sem=xr.at[slot],
            device_id={"gz": 1 - c}, device_id_type=MESH)

    barrier = pltpu.get_barrier_semaphore()

    @pl.when(z < Z - 1)
    def _():
        pl.semaphore_signal(barrier, inc=1, device_id={"gx": z + 1}, device_id_type=MESH)

    @pl.when(z > 0)
    def _():
        pl.semaphore_signal(barrier, inc=1, device_id={"gx": z - 1}, device_id_type=MESH)

    pl.semaphore_signal(barrier, inc=1, device_id={"gz": 1 - c}, device_id_type=MESH)
    peers = 1 + (z > 0).astype(jnp.int32) + (z < Z - 1).astype(jnp.int32)
    pl.semaphore_wait(barrier, peers)

    own = pltpu.make_async_copy(x_ref, place(z, c), own_sem)

    for k in range(Z - 1):
        @pl.when((z < Z - 1) & (z - k >= 0))
        def _():
            right(k).start()

        @pl.when((z > 0) & (z + k < Z))
        def _():
            left(k).start()

        if k == 0:
            own.start()
            cross(z, 0, x_ref).start()

        split(k * len(pieces) // (Z - 1), (k + 1) * len(pieces) // (Z - 1))

        @pl.when(z - 1 - k >= 0)
        def _():
            right_in(k).wait_recv()
            cross(z - 1 - k, 1 + k).start()

        @pl.when(z + 1 + k < Z)
        def _():
            left_in(k).wait_recv()
            cross(z + 1 + k, Z + k).start()

    save(len(pieces) - 1).wait()
    own.wait()
    cross(z, 0, x_ref).wait_send()
    cross_in(z, 0).wait_recv()
    for k in range(Z - 1):
        @pl.when((z < Z - 1) & (z - k >= 0))
        def _():
            right(k).wait_send()

        @pl.when((z > 0) & (z + k < Z))
        def _():
            left(k).wait_send()

        @pl.when(z - 1 - k >= 0)
        def _():
            cross(z - 1 - k, 1 + k).wait_send()
            cross_in(z - 1 - k, 1 + k).wait_recv()

        @pl.when(z + 1 + k < Z)
        def _():
            cross(z + 1 + k, Z + k).wait_send()
            cross_in(z + 1 + k, Z + k).wait_recv()


def gather_prompt(x, gate_up):
    Z, C, N = lax.axis_size("gx"), lax.axis_size("gz"), lax.axis_size("gy")
    rows, depth = x.shape
    sizes = chunk_sizes(gate_up.shape[2])
    cut = gate_up.shape[0] // 4
    count = 4 * len(sizes)
    sems = pltpu.SemaphoreType.DMA((Z - 1,))
    cross_sems = pltpu.SemaphoreType.DMA((2 * Z - 1,))
    split_sems = pltpu.SemaphoreType.DMA((count,))
    out = pl.pallas_call(
        functools.partial(gather_kernel, Z, C, N, sizes),
        out_shape=[jax.ShapeDtypeStruct((Z * C * rows, depth), x.dtype)] + [
            jax.ShapeDtypeStruct((gate_up.shape[0], 2, size), gate_up.dtype) for size in sizes],
        in_specs=[pl.BlockSpec(memory_space=pl.ANY)] * 2,
        out_specs=[pl.BlockSpec(memory_space=pltpu.VMEM)] + [
            pl.BlockSpec(memory_space=pl.ANY)] * len(sizes),
        scratch_shapes=[
            pltpu.SemaphoreType.DMA, sems, sems, sems, sems, cross_sems, cross_sems,
            pltpu.VMEM((4, cut, 2, max(sizes)), gate_up.dtype), split_sems, split_sems],
        compiler_params=pltpu.CompilerParams(
            collective_id=0, has_side_effects=True, vmem_limit_bytes=40 * 2**20),
        name="gather_prompt",
    )(x, gate_up)
    return out[0], out[1:]


def attention_kernel(scale, lens_ref, offset_ref, q_ref, kv_ref, num_ref, stat_ref):
    step = pl.program_id(0)
    per_step, slots, width = kv_ref.shape
    half = width // 2
    wide = q_ref.shape[1]
    per_head = wide // KVH
    row = lax.broadcasted_iota(jnp.int32, (wide, half), 0) // per_head
    col = lax.broadcasted_iota(jnp.int32, (wide, half), 1) // HD
    same = row == col
    position = offset_ref[0] + lax.broadcasted_iota(jnp.int32, (slots, wide), 0)
    for i in range(per_step):
        q = q_ref[i]
        spread = jnp.where(same, jnp.concatenate([q] * KVH, axis=1), jnp.zeros((), q.dtype))
        scores = lax.dot_general(
            kv_ref[i, :, :half], spread, (((1,), (1,)), ((), ())),
            preferred_element_type=jnp.float32) * scale
        visible = position < lens_ref[step * per_step + i]
        masked = jnp.where(visible, scores, lowest)
        top = jnp.max(masked, axis=0, keepdims=True)
        probs = jnp.where(visible, jnp.exp(masked - top), 0.0)
        for k, rest in enumerate((top, jnp.sum(probs, axis=0, keepdims=True))):
            for j in range(3):
                term = rest.astype(jnp.bfloat16).astype(jnp.float32)
                stat_ref[i, 3 * k + j:3 * k + j + 1, :] = term
                rest = rest - term
        full = lax.dot_general(
            probs.astype(jnp.bfloat16), kv_ref[i, :, half:], (((0,), (0,)), ((), ())),
            preferred_element_type=jnp.float32)
        for g in range(KVH):
            lo = g * per_head
            num_ref[i, lo:lo + per_head, :] = full[
                lo:lo + per_head, g * HD:(g + 1) * HD].astype(num_ref.dtype)


def attention(q, kv, lengths, offset):
    sequences, slots, width = kv.shape
    wide = q.shape[1]
    per_step = 4 if sequences % 4 == 0 else 1
    return pl.pallas_call(
        functools.partial(attention_kernel, 1.0 / math.sqrt(HD)),
        out_shape=(
            jax.ShapeDtypeStruct((sequences, wide, HD), jnp.bfloat16),
            jax.ShapeDtypeStruct((sequences, 6, wide), jnp.float32),
        ),
        grid_spec=pltpu.PrefetchScalarGridSpec(
            num_scalar_prefetch=2,
            grid=(sequences // per_step,),
            in_specs=[
                pl.BlockSpec((per_step, wide, HD), lambda i, a, b: (i, 0, 0)),
                pl.BlockSpec((per_step, slots, width), lambda i, a, b: (i, 0, 0)),
            ],
            out_specs=[
                pl.BlockSpec((per_step, wide, HD), lambda i, a, b: (i, 0, 0)),
                pl.BlockSpec((per_step, 6, wide), lambda i, a, b: (i, 0, 0)),
            ],
        ),
        cost_estimate=pl.CostEstimate(
            flops=sequences * slots * wide * width * 2,
            bytes_accessed=sequences * slots * width * 2,
            transcendentals=sequences * slots * wide),
        name="slot_attention",
    )(lengths, offset, q, kv)


def shifted(x, axes, k):
    n = lax.axis_size(axes)
    return lax.ppermute(x, axes, [(i, (i + k) % n) for i in range(n)])


def chunk_sizes(columns):
    tiles = columns // 128
    count = max(1, tiles // 4)
    sizes = [tiles // count] * count
    sizes[-1] += tiles - sum(sizes)
    return [128 * size for size in sizes]


def projections(x_all, weights, between, late):
    N = lax.axis_size("gy")
    rows = x_all.shape[0] // N
    chunks = range(len(weights))

    def product(x, c):
        part = lax.dot_general(
            x, weights[c], (((1,), (0,)), ((), ())),
            preferred_element_type=jnp.float32)
        return jnp.transpose(part, (1, 0, 2)).astype(jnp.bfloat16)

    arrived = []
    for c in chunks:
        parts = [product(x_all[(k - 1) * rows:k * rows], c) for k in range(1, N)]
        arrived.append([shifted(part, "gy", k + 1) for k, part in enumerate(parts)])
    x_all, parts, between = lax.optimization_barrier((x_all, parts, between))
    x_keep = x_all[(N - 1) * rows:]
    hidden = []
    for c in chunks:
        total = product(x_keep, c).astype(jnp.float32)
        for other in arrived[c]:
            total = total + other.astype(jnp.float32)
        if c == max(0, len(weights) - 2):
            total, late = lax.optimization_barrier((total, late))
        hidden.append((jax.nn.silu(total[0]) * total[1]).astype(jnp.bfloat16))
    return jnp.concatenate(hidden, axis=1), between, late


def join_kernel(n, q_ref, k_ref, v_ref, *refs):
    part_refs, out_ref = refs[:n], refs[n]
    S, B, width = q_ref.shape
    heads = width // HD

    def stat(ref, s, h, k):
        terms = [
            ref[s, :, width + (3 * k + j) * heads + h:width + (3 * k + j) * heads + h + 1]
            for j in range(3)]
        return sum(term.astype(jnp.float32) for term in terms)

    scale = 1.0 / math.sqrt(HD)
    for s in range(S):
        keys = [k_ref[t].astype(jnp.float32) for t in range(s + 1)]
        values = [v_ref[t].astype(jnp.float32) for t in range(s + 1)]
        for h in range(width // HD):
            lanes = slice(h * HD, (h + 1) * HD)
            q = q_ref[s, :, lanes].astype(jnp.float32)
            fresh = [jnp.sum(q * key, axis=-1, keepdims=True) * scale for key in keys]
            tops = [stat(r, s, h, 0) for r in part_refs]
            top = functools.reduce(jnp.maximum, fresh + tops)
            denominator = jnp.zeros_like(top)
            numerator = jnp.zeros_like(q)
            for score, value in zip(fresh, values):
                prob = jnp.exp(score - top)
                denominator = denominator + prob
                numerator = numerator + prob.astype(jnp.bfloat16).astype(jnp.float32) * value
            for local, part in zip(tops, part_refs):
                factor = jnp.exp(local - top)
                denominator = denominator + stat(part, s, h, 1) * factor
                numerator = numerator + part[s, :, lanes].astype(jnp.float32) * factor
            out_ref[s, :, lanes] = (numerator / denominator).astype(out_ref.dtype)


def join(q, k, v, parts):
    n = len(parts)
    return pl.pallas_call(
        functools.partial(join_kernel, n),
        out_shape=jax.ShapeDtypeStruct(q.shape, q.dtype),
        in_specs=[pl.BlockSpec(memory_space=pltpu.VMEM)] * (3 + n),
        out_specs=pl.BlockSpec(memory_space=pltpu.VMEM),
        cost_estimate=pl.CostEstimate(
            flops=8 * n * q.size, bytes_accessed=2 * (n + 2) * q.size, transcendentals=0),
        name="join_parts",
    )(q, k, v, *parts)


def on_device(prompt_rows, gate_up, queries, new_kv, kv_cache, lengths):
    both = ("gx", "gz")
    n = lax.axis_size(both)
    me = lax.axis_index(both)
    S, B, width = queries.shape
    heads = width // HD
    group = n * heads // KVH
    per = n // KVH

    x_all, weights = gather_prompt(prompt_rows, gate_up)
    x_all, late_queries = lax.optimization_barrier((x_all, queries))

    slots_of = jnp.zeros((n, S, B, width), queries.dtype)
    slots_of = lax.dynamic_update_index_in_dim(slots_of, late_queries, me, 0)
    for k in range(1, n):
        slots_of = lax.dynamic_update_index_in_dim(
            slots_of, shifted(late_queries, both, k), lax.rem(me - k + n, n), 0)
    q = slots_of.reshape(KVH, per, S, B, heads, HD)
    q = jnp.transpose(q, (3, 0, 2, 1, 4, 5)).reshape(B, KVH * S * group, HD)

    offset = (me * kv_cache.shape[1]).astype(jnp.int32).reshape(1)
    num, stat = attention(q, kv_cache, lengths, offset)
    hidden_units, (num, stat), queries = projections(x_all, weights, (num, stat), queries)
    num = jnp.transpose(num.reshape(B, KVH, S, per, heads, HD), (1, 3, 2, 0, 4, 5))
    num = num.reshape(n, S, B, width)
    stat = stat.astype(jnp.bfloat16).reshape(B, 6, KVH, S, per, heads)
    stat = jnp.transpose(stat, (2, 4, 3, 0, 1, 5)).reshape(n, S, B, 6 * heads)
    stat = jnp.pad(stat, ((0, 0), (0, 0), (0, 0), (0, 128 - 6 * heads)))
    parts = jnp.concatenate([num, stat], axis=-1)

    def take(i):
        return lax.dynamic_index_in_dim(parts, i, 0, False)

    held = [take(me)] + [
        shifted(take(lax.rem(me + k, n)), both, k) for k in range(1, n)]

    head_at = me * heads // group
    fresh = new_kv.reshape(S, B, 2, KVH, HD)
    keys = lax.dynamic_index_in_dim(fresh[:, :, 0], head_at, 2, False)
    values = lax.dynamic_index_in_dim(fresh[:, :, 1], head_at, 2, False)
    attended = join(queries, keys, values, held)
    return (hidden_units, attended)


def solution(mesh):
    return jax.shard_map(
        on_device,
        mesh=mesh,
        in_specs=(
            P(("groups", "gx", "gz"), "gy"),
            P("gy", None, ("gx", "gz")),
            P(None, ("groups", "gy"), ("gx", "gz")),
            P(None, ("groups", "gy"), None),
            P(("groups", "gy"), ("gx", "gz"), None),
            P(("groups", "gy")),
        ),
        out_specs=(P(("groups", "gy"), ("gx", "gz")), P(None, ("groups", "gy"), ("gx", "gz"))),
        check_vma=False,
    )
```

```python
import functools
import math

import jax
import jax.numpy as jnp
from jax import lax
from jax.experimental import pallas as pl
from jax.experimental.pallas import tpu as pltpu
from jax.sharding import PartitionSpec as P

KVH = 4
HD = 128
MESH = pl.DeviceIdType.MESH

lowest = -1e30


def gather_kernel(Z, C, N, sizes, x_ref, w_ref, out_ref, *rest):
    w_outs = rest[:len(sizes)]
    own_sem, rs, rr, ls, lr, xs, xr, buf, in_sems, out_sems = rest[len(sizes):]
    depth = buf.shape[1]
    cuts = w_ref.shape[0] // depth
    pieces = [(c, i) for c in range(len(sizes)) for i in range(cuts)]
    slots = buf.shape[0]

    def load(p):
        c, i = pieces[p]
        return pltpu.make_async_copy(
            w_ref.at[pl.ds(i * depth, depth), :, pl.ds(sum(sizes[:c]), sizes[c])],
            buf.at[p % slots, :, :, pl.ds(0, sizes[c])], in_sems.at[p])

    def save(p):
        c, i = pieces[p]
        return pltpu.make_async_copy(
            buf.at[p % slots, :, :, pl.ds(0, sizes[c])],
            w_outs[c].at[pl.ds(i * depth, depth)], out_sems.at[p])

    def split(first, last):
        for p in range(first, last):
            load(p).wait()
            save(p).start()
            if p >= 1:
                save(p - 1).wait()
            if p + slots - 1 < len(pieces):
                load(p + slots - 1).start()

    for p in range(min(slots - 1, len(pieces))):
        load(p).start()
    z = lax.axis_index("gx")
    c = lax.axis_index("gz")
    y = lax.axis_index("gy")
    n = Z * C
    rows = x_ref.shape[0]

    def place(zz, cc):
        p = lax.rem(zz * C + cc - (y + 1) * (n // N) + 2 * n, n)
        return out_ref.at[pl.ds(pl.multiple_of(p * rows, rows), rows)]

    def right(k):
        src = x_ref if k == 0 else place(z - k, c)
        return pltpu.make_async_remote_copy(
            src_ref=src, dst_ref=place(z - k, c), send_sem=rs.at[k], recv_sem=rr.at[k],
            device_id={"gx": z + 1}, device_id_type=MESH)

    def left(k):
        src = x_ref if k == 0 else place(z + k, c)
        return pltpu.make_async_remote_copy(
            src_ref=src, dst_ref=place(z + k, c), send_sem=ls.at[k], recv_sem=lr.at[k],
            device_id={"gx": z - 1}, device_id_type=MESH)

    def right_in(k):
        return pltpu.make_async_remote_copy(
            src_ref=x_ref, dst_ref=place(z - 1 - k, c), send_sem=rs.at[k], recv_sem=rr.at[k],
            device_id={"gx": z - 1}, device_id_type=MESH)

    def left_in(k):
        return pltpu.make_async_remote_copy(
            src_ref=x_ref, dst_ref=place(z + 1 + k, c), send_sem=ls.at[k], recv_sem=lr.at[k],
            device_id={"gx": z + 1}, device_id_type=MESH)

    def cross(zz, slot, src=None):
        block = place(zz, c)
        return pltpu.make_async_remote_copy(
            src_ref=block if src is None else src, dst_ref=block,
            send_sem=xs.at[slot], recv_sem=xr.at[slot],
            device_id={"gz": 1 - c}, device_id_type=MESH)

    def cross_in(zz, slot):
        return pltpu.make_async_remote_copy(
            src_ref=x_ref, dst_ref=place(zz, 1 - c),
            send_sem=xs.at[slot], recv_sem=xr.at[slot],
            device_id={"gz": 1 - c}, device_id_type=MESH)

    barrier = pltpu.get_barrier_semaphore()

    @pl.when(z < Z - 1)
    def _():
        pl.semaphore_signal(barrier, inc=1, device_id={"gx": z + 1}, device_id_type=MESH)

    @pl.when(z > 0)
    def _():
        pl.semaphore_signal(barrier, inc=1, device_id={"gx": z - 1}, device_id_type=MESH)

    pl.semaphore_signal(barrier, inc=1, device_id={"gz": 1 - c}, device_id_type=MESH)
    peers = 1 + (z > 0).astype(jnp.int32) + (z < Z - 1).astype(jnp.int32)
    pl.semaphore_wait(barrier, peers)

    own = pltpu.make_async_copy(x_ref, place(z, c), own_sem)

    for k in range(Z - 1):
        @pl.when((z < Z - 1) & (z - k >= 0))
        def _():
            right(k).start()

        @pl.when((z > 0) & (z + k < Z))
        def _():
            left(k).start()

        if k == 0:
            own.start()
            cross(z, 0, x_ref).start()

        split(k * len(pieces) // (Z - 1), (k + 1) * len(pieces) // (Z - 1))

        @pl.when(z - 1 - k >= 0)
        def _():
            right_in(k).wait_recv()
            cross(z - 1 - k, 1 + k).start()

        @pl.when(z + 1 + k < Z)
        def _():
            left_in(k).wait_recv()
            cross(z + 1 + k, Z + k).start()

    save(len(pieces) - 1).wait()
    own.wait()
    cross(z, 0, x_ref).wait_send()
    cross_in(z, 0).wait_recv()
    for k in range(Z - 1):
        @pl.when((z < Z - 1) & (z - k >= 0))
        def _():
            right(k).wait_send()

        @pl.when((z > 0) & (z + k < Z))
        def _():
            left(k).wait_send()

        @pl.when(z - 1 - k >= 0)
        def _():
            cross(z - 1 - k, 1 + k).wait_send()
            cross_in(z - 1 - k, 1 + k).wait_recv()

        @pl.when(z + 1 + k < Z)
        def _():
            cross(z + 1 + k, Z + k).wait_send()
            cross_in(z + 1 + k, Z + k).wait_recv()


def gather_prompt(x, gate_up):
    Z, C, N = lax.axis_size("gx"), lax.axis_size("gz"), lax.axis_size("gy")
    rows, depth = x.shape
    sizes = chunk_sizes(gate_up.shape[2])
    cut = gate_up.shape[0] // 4
    count = 4 * len(sizes)
    sems = pltpu.SemaphoreType.DMA((Z - 1,))
    cross_sems = pltpu.SemaphoreType.DMA((2 * Z - 1,))
    split_sems = pltpu.SemaphoreType.DMA((count,))
    out = pl.pallas_call(
        functools.partial(gather_kernel, Z, C, N, sizes),
        out_shape=[jax.ShapeDtypeStruct((Z * C * rows, depth), x.dtype)] + [
            jax.ShapeDtypeStruct((gate_up.shape[0], 2, size), gate_up.dtype) for size in sizes],
        in_specs=[pl.BlockSpec(memory_space=pl.ANY)] * 2,
        out_specs=[pl.BlockSpec(memory_space=pltpu.VMEM)] + [
            pl.BlockSpec(memory_space=pl.ANY)] * len(sizes),
        scratch_shapes=[
            pltpu.SemaphoreType.DMA, sems, sems, sems, sems, cross_sems, cross_sems,
            pltpu.VMEM((4, cut, 2, max(sizes)), gate_up.dtype), split_sems, split_sems],
        compiler_params=pltpu.CompilerParams(
            collective_id=0, has_side_effects=True, vmem_limit_bytes=40 * 2**20),
        name="gather_prompt",
    )(x, gate_up)
    return out[0], out[1:]


def attention_kernel(scale, lens_ref, offset_ref, q_ref, kv_ref, num_ref, stat_ref):
    step = pl.program_id(0)
    per_step, slots, width = kv_ref.shape
    half = width // 2
    wide = q_ref.shape[1]
    per_head = wide // KVH
    row = lax.broadcasted_iota(jnp.int32, (wide, half), 0) // per_head
    col = lax.broadcasted_iota(jnp.int32, (wide, half), 1) // HD
    same = row == col
    position = offset_ref[0] + lax.broadcasted_iota(jnp.int32, (slots, wide), 0)
    for i in range(per_step):
        q = q_ref[i]
        spread = jnp.where(same, jnp.concatenate([q] * KVH, axis=1), jnp.zeros((), q.dtype))
        scores = lax.dot_general(
            kv_ref[i, :, :half], spread, (((1,), (1,)), ((), ())),
            preferred_element_type=jnp.float32) * scale
        visible = position < lens_ref[step * per_step + i]
        masked = jnp.where(visible, scores, lowest)
        top = jnp.max(masked, axis=0, keepdims=True)
        probs = jnp.where(visible, jnp.exp(masked - top), 0.0)
        for k, rest in enumerate((top, jnp.sum(probs, axis=0, keepdims=True))):
            for j in range(3):
                term = rest.astype(jnp.bfloat16).astype(jnp.float32)
                stat_ref[i, 3 * k + j:3 * k + j + 1, :] = term
                rest = rest - term
        full = lax.dot_general(
            probs.astype(jnp.bfloat16), kv_ref[i, :, half:], (((0,), (0,)), ((), ())),
            preferred_element_type=jnp.float32)
        for g in range(KVH):
            lo = g * per_head
            num_ref[i, lo:lo + per_head, :] = full[
                lo:lo + per_head, g * HD:(g + 1) * HD].astype(num_ref.dtype)


def attention(q, kv, lengths, offset):
    sequences, slots, width = kv.shape
    wide = q.shape[1]
    per_step = 4 if sequences % 4 == 0 else 1
    return pl.pallas_call(
        functools.partial(attention_kernel, 1.0 / math.sqrt(HD)),
        out_shape=(
            jax.ShapeDtypeStruct((sequences, wide, HD), jnp.bfloat16),
            jax.ShapeDtypeStruct((sequences, 6, wide), jnp.float32),
        ),
        grid_spec=pltpu.PrefetchScalarGridSpec(
            num_scalar_prefetch=2,
            grid=(sequences // per_step,),
            in_specs=[
                pl.BlockSpec((per_step, wide, HD), lambda i, a, b: (i, 0, 0)),
                pl.BlockSpec((per_step, slots, width), lambda i, a, b: (i, 0, 0)),
            ],
            out_specs=[
                pl.BlockSpec((per_step, wide, HD), lambda i, a, b: (i, 0, 0)),
                pl.BlockSpec((per_step, 6, wide), lambda i, a, b: (i, 0, 0)),
            ],
        ),
        cost_estimate=pl.CostEstimate(
            flops=sequences * slots * wide * width * 2,
            bytes_accessed=sequences * slots * width * 2,
            transcendentals=sequences * slots * wide),
        name="slot_attention",
    )(lengths, offset, q, kv)


def shifted(x, axes, k):
    n = lax.axis_size(axes)
    return lax.ppermute(x, axes, [(i, (i + k) % n) for i in range(n)])


def chunk_sizes(columns):
    tiles = columns // 128
    count = max(1, tiles // 4)
    sizes = [tiles // count] * count
    sizes[-1] += tiles - sum(sizes)
    return [128 * size for size in sizes]


def projections(x_all, weights, between, late):
    N = lax.axis_size("gy")
    rows = x_all.shape[0] // N
    chunks = range(len(weights))

    def product(x, c):
        part = lax.dot_general(
            x, weights[c], (((1,), (0,)), ((), ())),
            preferred_element_type=jnp.float32)
        return jnp.transpose(part, (1, 0, 2)).astype(jnp.bfloat16)

    arrived = []
    for c in chunks:
        parts = [product(x_all[(k - 1) * rows:k * rows], c) for k in range(1, N)]
        arrived.append([shifted(part, "gy", k + 1) for k, part in enumerate(parts)])
    x_all, parts, between = lax.optimization_barrier((x_all, parts, between))
    x_keep = x_all[(N - 1) * rows:]
    hidden = []
    for c in chunks:
        total = product(x_keep, c).astype(jnp.float32)
        for other in arrived[c]:
            total = total + other.astype(jnp.float32)
        if c == max(0, len(weights) - 2):
            total, late = lax.optimization_barrier((total, late))
        hidden.append((jax.nn.silu(total[0]) * total[1]).astype(jnp.bfloat16))
    return jnp.concatenate(hidden, axis=1), between, late


def join_kernel(n, q_ref, k_ref, v_ref, *refs):
    part_refs, out_ref = refs[:n], refs[n]
    S, B, width = q_ref.shape
    heads = width // HD

    def stat(ref, s):
        tail = ref[s, :, width:width + 128].astype(jnp.float32)
        terms = [tail[:, j * heads:(j + 1) * heads] for j in range(6)]
        return terms[0] + terms[1] + terms[2], terms[3] + terms[4] + terms[5]

    scale = 1.0 / math.sqrt(HD)
    for s in range(S):
        keys = [k_ref[t].astype(jnp.float32) for t in range(s + 1)]
        values = [v_ref[t].astype(jnp.float32) for t in range(s + 1)]
        stats = [stat(r, s) for r in part_refs]
        peak = functools.reduce(jnp.maximum, [t for t, _ in stats])
        factors = [jnp.exp(t - peak) for t, _ in stats]
        total = sum(d * f for (_, d), f in zip(stats, factors))
        for h in range(heads):
            lanes = slice(h * HD, (h + 1) * HD)
            q = q_ref[s, :, lanes].astype(jnp.float32)
            fresh = [jnp.sum(q * key, axis=-1, keepdims=True) * scale for key in keys]
            old = peak[:, h:h + 1]
            top = functools.reduce(jnp.maximum, fresh, old)
            numerator = jnp.zeros_like(q)
            for factor, part in zip(factors, part_refs):
                numerator = numerator + part[s, :, lanes].astype(jnp.float32) * factor[:, h:h + 1]
            shrink = jnp.exp(old - top)
            numerator = numerator * shrink
            denominator = total[:, h:h + 1] * shrink
            for score, value in zip(fresh, values):
                prob = jnp.exp(score - top)
                denominator = denominator + prob
                numerator = numerator + prob.astype(jnp.bfloat16).astype(jnp.float32) * value
            out_ref[s, :, lanes] = (numerator / denominator).astype(out_ref.dtype)


def join(q, k, v, parts):
    n = len(parts)
    return pl.pallas_call(
        functools.partial(join_kernel, n),
        out_shape=jax.ShapeDtypeStruct(q.shape, q.dtype),
        in_specs=[pl.BlockSpec(memory_space=pltpu.VMEM)] * (3 + n),
        out_specs=pl.BlockSpec(memory_space=pltpu.VMEM),
        cost_estimate=pl.CostEstimate(
            flops=8 * n * q.size, bytes_accessed=2 * (n + 2) * q.size, transcendentals=0),
        name="join_parts",
    )(q, k, v, *parts)


def on_device(prompt_rows, gate_up, queries, new_kv, kv_cache, lengths):
    both = ("gx", "gz")
    n = lax.axis_size(both)
    me = lax.axis_index(both)
    S, B, width = queries.shape
    heads = width // HD
    group = n * heads // KVH
    per = n // KVH

    x_all, weights = gather_prompt(prompt_rows, gate_up)
    x_all, late_queries = lax.optimization_barrier((x_all, queries))

    slots_of = jnp.zeros((n, S, B, width), queries.dtype)
    slots_of = lax.dynamic_update_index_in_dim(slots_of, late_queries, me, 0)
    for k in range(1, n):
        slots_of = lax.dynamic_update_index_in_dim(
            slots_of, shifted(late_queries, both, k), lax.rem(me - k + n, n), 0)
    q = slots_of.reshape(KVH, per, S, B, heads, HD)
    q = jnp.transpose(q, (3, 0, 2, 1, 4, 5)).reshape(B, KVH * S * group, HD)

    offset = (me * kv_cache.shape[1]).astype(jnp.int32).reshape(1)
    num, stat = attention(q, kv_cache, lengths, offset)
    hidden_units, (num, stat), queries = projections(x_all, weights, (num, stat), queries)
    num = jnp.transpose(num.reshape(B, KVH, S, per, heads, HD), (1, 3, 2, 0, 4, 5))
    num = num.reshape(n, S, B, width)
    stat = stat.astype(jnp.bfloat16).reshape(B, 6, KVH, S, per, heads)
    stat = jnp.transpose(stat, (2, 4, 3, 0, 1, 5)).reshape(n, S, B, 6 * heads)
    stat = jnp.pad(stat, ((0, 0), (0, 0), (0, 0), (0, 128 - 6 * heads)))
    parts = jnp.concatenate([num, stat], axis=-1)

    def take(i):
        return lax.dynamic_index_in_dim(parts, i, 0, False)

    held = [take(me)] + [
        shifted(take(lax.rem(me + k, n)), both, k) for k in range(1, n)]

    head_at = me * heads // group
    fresh = new_kv.reshape(S, B, 2, KVH, HD)
    keys = lax.dynamic_index_in_dim(fresh[:, :, 0], head_at, 2, False)
    values = lax.dynamic_index_in_dim(fresh[:, :, 1], head_at, 2, False)
    attended = join(queries, keys, values, held)
    return (hidden_units, attended)


def solution(mesh):
    return jax.shard_map(
        on_device,
        mesh=mesh,
        in_specs=(
            P(("groups", "gx", "gz"), "gy"),
            P("gy", None, ("gx", "gz")),
            P(None, ("groups", "gy"), ("gx", "gz")),
            P(None, ("groups", "gy"), None),
            P(("groups", "gy"), ("gx", "gz"), None),
            P(("groups", "gy")),
        ),
        out_specs=(P(("groups", "gy"), ("gx", "gz")), P(None, ("groups", "gy"), ("gx", "gz"))),
        check_vma=False,
    )
```
